256 devices in a mesh: gx: 8 (over x, core), gy: 32 (over z, y).
Axes of the slice: x: 4, y: 4, z: 8, core: 2. Of those that a mesh axis runs over, the one named last changes fastest.
Arguments:
- volume: bfloat16 [64, 256, 2, 256], P('gx', 'gy'), may hold values from -6 to 6
- first_weight: bfloat16 [6912, 256], replicated, may hold values from -0.078125 to 0.078125
- second_weight: bfloat16 [6912, 256], replicated, may hold values from -0.078125 to 0.078125
- cotangent: bfloat16 [64, 256, 2, 256], P('gx', 'gy'), may hold values from -6 to 6
Outputs:
- output: bfloat16 [64, 256, 2, 256], P('gx', 'gy')
- volume_grad: bfloat16 [64, 256, 2, 256], P('gx', 'gy')
- second_grad: float32 [1769472], P(('gx', 'gy'))
The draws below stay inside these ranges and needn't reach their ends.
All inputs are finite; a program needn't handle non-finite values.
Results may differ from the reference program's by a relative error of at most 0.015.
Values may be sent and summed in bfloat16 or wider, within the bound.
A program may use at most 64 MiB of HBM per device.

```python
import jax
import jax.numpy as jnp
from jax import lax

C = 256
KTAPS = 27
SLAB = 2
NX = 64
NY = 256


def block_levels(stream_key, shape, pieces, low, largest):
    def one(axis_at, shards_of):
        steps = jax.random.uniform(jax.random.fold_in(jax.random.fold_in(stream_key, 6), axis_at), (shards_of,), jnp.float32, low / len(pieces), largest / len(pieces))
        return jnp.repeat(jnp.exp(steps), shape[axis_at] // shards_of).reshape((-1,) + (1,) * (len(shape) - axis_at - 1))

    factor_of = one(*pieces[0])
    for cut in pieces[1:]:
        factor_of = factor_of * one(*cut)
    return factor_of


def bell_draw(key, shape, spread, limit, split=(), held_as=jnp.bfloat16):
    loudness = block_levels(key, shape, split, -0.22, 0.18) if split else 1.0
    values = jax.random.normal(key, shape, jnp.float32) * spread * loudness
    return jnp.minimum(jnp.maximum(values, -limit), limit).astype(held_as)


def setup_inputs(seed: int = 0) -> dict:
    keys = jax.random.split(jax.random.key(seed), 5)
    return {
        "volume": bell_draw(keys[0], (NX, NY, SLAB, C), 1.0, 6.0, ((0, 8), (1, 32))),
        "first_weight": bell_draw(keys[1], (KTAPS * C, C), (KTAPS * C) ** -0.5, 0.078125),
        "second_weight": bell_draw(keys[2], (KTAPS * C, C), (KTAPS * C) ** -0.5, 0.078125),
        "cotangent": bell_draw(keys[3], (NX, NY, SLAB, C), 1.0, 6.0, ((0, 8), (1, 32))),
    }


def pad_field(field):
    wrapped = jnp.pad(field, ((1, 1), (1, 1), (0, 0), (0, 0)), mode='wrap')
    return jnp.pad(wrapped, ((0, 0), (0, 0), (1, 1), (0, 0)))

def correlate(field, kernel):
    padded = pad_field(field.astype(jnp.float32))
    chans = field.shape[3]
    weights = kernel.astype(jnp.float32).reshape(3, 3, 3, chans, kernel.shape[1])
    result = lax.conv_general_dilated(padded[None], weights, (1, 1, 1), 'VALID', dimension_numbers=('NDHWC', 'DHWIO', 'NDHWC'), precision=lax.Precision.HIGHEST)
    return result[0]

def weight_grad(source, grad):
    padded = pad_field(source.astype(jnp.float32))
    gfull = grad.astype(jnp.float32)
    sx, sy, sz = (grad.shape[0], grad.shape[1], grad.shape[2])
    blocks = []
    for a in range(3):
        for b in range(3):
            for e in range(3):
                piece = padded[a:a + sx, b:b + sy, e:e + sz, :]
                blocks.append(jnp.einsum('xyzc,xyzd->cd', piece, gfull, precision=lax.Precision.HIGHEST))
    scale = 1.0 / jnp.sqrt(jnp.float32(NX * NY * SLAB))
    return (jnp.concatenate(blocks, axis=0) * scale).reshape(-1)

def flipped(kernel):
    chans = kernel.shape[1]
    weights = kernel.reshape(3, 3, 3, chans, chans)[::-1, ::-1, ::-1]
    return jnp.transpose(weights, (0, 1, 2, 4, 3)).reshape(KTAPS * chans, chans)

def reference(volume, first_weight, second_weight, cotangent):
    pre = correlate(volume, first_weight)
    hidden = jax.nn.silu(pre).astype(jnp.bfloat16)
    output = correlate(hidden, second_weight).astype(jnp.bfloat16)
    second_grad = weight_grad(hidden, cotangent)
    back = correlate(cotangent, flipped(second_weight))
    sig = jax.nn.sigmoid(pre)
    through = (back * sig * (1.0 + pre * (1.0 - sig))).astype(jnp.bfloat16)
    volume_grad = correlate(through, flipped(first_weight)).astype(jnp.bfloat16)
    return (output, volume_grad, second_grad)
```

```python
import jax
import jax.numpy as jnp
import numpy as np
from jax import lax
from jax.experimental import pallas as pl
from jax.experimental.pallas import tpu as pltpu
from jax.sharding import PartitionSpec as P

C = 256
NGX = 8
NGY = 32
OWN = 64
ROWS = 27
PAD = 32
SLOTS = 5
F32 = jnp.float32
BF16 = jnp.bfloat16
MESH = pl.DeviceIdType.MESH


def strip_matrix():
    m = np.zeros((96, OWN), np.float32)
    for x in range(8):
        for j in range(2):
            m[x * 2 + j, x * 8 + 6 + j] = 1
            m[16 + x * 2 + j, x * 8 + j] = 1
    for i, (x0, y0) in enumerate(((6, 6), (6, 0), (0, 6), (0, 0))):
        for k in range(2):
            for j in range(2):
                m[32 + 16 * i + 2 * k + j, (x0 + k) * 8 + y0 + j] = 1
    return m


def window_matrices():
    own = np.zeros((192, OWN), np.float32)
    got = np.zeros((192, 128), np.float32)
    for xi in range(12):
        for yj in range(16):
            if 10 <= yj < 14:
                continue
            x, y, r = xi - 2, (yj if yj < 10 else yj - 16), xi * 16 + yj
            xs = -1 if x < 0 else (1 if x > 7 else 0)
            ys = -1 if y < 0 else (1 if y > 7 else 0)
            xr, yr = (x + 2 if xs < 0 else x - 8), (y + 2 if ys < 0 else y - 8)
            if xs == 0 and ys == 0:
                own[r, x * 8 + y] = 1
            elif ys == 0:
                got[r, (0 if xs < 0 else 16) + xr * 8 + y] = 1
            elif xs == 0:
                got[r, (32 if ys < 0 else 48) + x * 2 + yr] = 1
            else:
                base = 64 + (0 if xs < 0 else 32) + (0 if ys < 0 else 16)
                got[r, base + xr * 2 + yr] = 1
    return own, got


def dot(a, b):
    return jnp.dot(a, b, preferred_element_type=F32)


def dot_t(a, b):
    return lax.dot_general(a, b, (((1,), (1,)), ((), ())), preferred_element_type=F32)


def cyclic(x, shift):
    rows = x.shape[0]
    return pltpu.roll(x.reshape(rows // 16, 16, x.shape[1]), shift % 16, axis=1).reshape(rows, x.shape[1])


def corr(src, w, rows, z, flip):
    total = None
    for b in range(3):
        acc = None
        for a in range(3):
            if flip:
                tap = ((2 - a) * 3 + (2 - b)) * 3
                term = None
                for zi in range(2):
                    e = tap + 1 + z - zi
                    d = dot_t(src[16 * a : 16 * a + rows, zi * C : (zi + 1) * C], w[e * C : (e + 1) * C, :])
                    term = d if term is None else term + d
            else:
                tap = (a * 3 + b) * 3 + 1 - z
                term = dot(src[16 * a : 16 * a + rows, :], w[tap * C : (tap + 2) * C, :])
            acc = term if acc is None else acc + term
        if b != 1:
            acc = cyclic(acc, 1 - b)
        total = acc if total is None else total + acc
    return total


def own_rows(x, first):
    return x.reshape(x.shape[0] // 16, 16, C)[first : first + 8, 0:8, :].reshape(OWN, C)


def kernel(
    v_ref, c_ref, w1_hbm, w2_hbm, p_ref, qo_ref, qs_ref,
    out_ref, vg_ref, sg_ref,
    w1, w2, strips, got, ext, hext, text, pre, cg, cs, cgf, csf, hg, rbuf, grad, chunk, land,
    wsem, hsend, hrecv, csend, crecv, ssend, srecv, gsend, grecv, rsend, rrecv,
):
    gx, gy = lax.axis_index("gx"), lax.axis_index("gy")

    def at(dx, dy):
        return (lax.rem(gx + dx + NGX, NGX), lax.rem(gy + dy + NGY, NGY))

    barrier = pltpu.get_barrier_semaphore()
    near = [(1, 0), (-1, 0), (0, 1), (0, -1), (1, 1), (1, -1), (-1, 1), (-1, -1)]
    for dx, dy in near:
        pl.semaphore_signal(barrier, inc=1, device_id=at(dx, dy), device_id_type=MESH)
    for k in range(2, NGX - 1):
        pl.semaphore_signal(barrier, inc=1, device_id=at(k, 0), device_id_type=MESH)

    @pl.loop(2, NGY - 1)
    def _(k):
        pl.semaphore_signal(barrier, inc=1, device_id=at(0, k), device_id_type=MESH)

    copies_w = [
        pltpu.make_async_copy(w1_hbm, w1, wsem.at[0]),
        pltpu.make_async_copy(w2_hbm, w2, wsem.at[1]),
    ]
    for c in copies_w:
        c.start()
    for i, ref in enumerate((v_ref, c_ref)):
        strips[i] = dot(p_ref[...], ref[...]).astype(BF16)
    pl.semaphore_wait(barrier, len(near) + (NGX - 3) + (NGY - 3))

    halo = []
    for i, ref in enumerate((v_ref, c_ref)):
        sources = [ref.at[48:64], ref.at[0:16]] + [strips.at[i, 16 * n : 16 * n + 16] for n in range(6)]
        row = []
        for n, (dx, dy) in enumerate(near):
            row.append(pltpu.make_async_remote_copy(
                src_ref=sources[n], dst_ref=got.at[i, 16 * n : 16 * n + 16],
                send_sem=hsend.at[i, n], recv_sem=hrecv.at[i, n],
                device_id=at(dx, dy), device_id_type=MESH))
            row[-1].start()
        halo.append(row)

    def to_ring(src, dst, send, recv):
        out = []
        for k in range(1, NGX):
            out.append(pltpu.make_async_remote_copy(
                src_ref=src, dst_ref=dst.at[gx], send_sem=send.at[k], recv_sem=recv.at[k],
                device_id=at(k, 0), device_id_type=MESH))
            out[-1].start()
        return out

    craw = to_ring(c_ref, cg, csend, crecv)
    cg[gx] = c_ref[...]

    for n in range(8):
        halo[0][n].wait_recv()
    ext[0] = (dot(qo_ref[...], v_ref[...]) + dot(qs_ref[...], got[0])).astype(BF16)
    for n in range(8):
        halo[1][n].wait_recv()
    cstrip = to_ring(got.at[1, 32:64], cs, ssend, srecv)
    cs[gx] = got[1, 32:64, :]
    ext[1] = (dot(qo_ref[...], c_ref[...]) + dot(qs_ref[...], got[1])).astype(BF16)

    copies_w[0].wait()
    tall = []
    for z in range(2):
        p = corr(ext.at[0], w1, 160, z, False)
        pre[:, z * C : (z + 1) * C] = p
        h = p / (1.0 + jnp.exp(-p))
        hext[:, z * C : (z + 1) * C] = h.astype(BF16)
        tall.append(own_rows(h, 1))
    hg[gx] = jnp.transpose(jnp.concatenate(tall, axis=0)).astype(BF16)
    hid = to_ring(hg.at[gx], hg, gsend, grecv)

    for c in craw + cstrip:
        c.wait_recv()
    for g in range(NGX):
        for z in range(2):
            cgf[z, 64 * g : 64 * g + 64, :] = cg[g, :, z * C : (z + 1) * C].astype(F32)
            csf[z, 32 * g : 32 * g + 32, :] = cs[g, :, z * C : (z + 1) * C].astype(F32)

    first = (gx * ROWS * NGY) // C
    offset = gx * ROWS * NGY - first * C
    lane8 = lax.broadcasted_iota(jnp.int32, (8, C), 0)

    @pl.loop(0, SLOTS * NGX)
    def _(it):
        s = it // NGX
        g = it - s * NGX
        t = jnp.minimum(first + s, 26)
        a = t // 9
        b = (t // 3) - 3 * a
        e = t - 9 * a - 3 * b
        edge = jnp.where(b == 0, 7, jnp.where(b == 2, 0, 8))
        turn = jnp.where(b == 0, 7, jnp.where(b == 2, 1, 0))
        side = jnp.where(b == 0, 16, 1)
        for z in range(2):
            zs = jnp.where(e == 0, 1, 0) if z == 0 else jnp.where(e == 2, 0, 1)
            keep = (e < 2) if z == 0 else (e > 0)
            for pair in range(4):
                blocks = []
                for xl in (2 * pair, 2 * pair + 1):
                    xs = lax.rem(g * 8 + xl + 1 - a + 64, 64)
                    gs = xs // 8
                    block = cgf[zs, pl.ds(pl.multiple_of(xs * 8, 8), 8), :]
                    line = csf[zs, pl.ds(gs * 32 + side + 2 * (xs - gs * 8), 1), :]
                    block = pltpu.roll(block, turn, axis=0)
                    block = jnp.where(lane8 == edge, line, block)
                    blocks.append(jnp.where(keep, block, 0.0))
                rbuf[s, pl.ds(pl.multiple_of(g * 128 + z * 64 + pair * 16, 16), 16), :] = (
                    jnp.concatenate(blocks, axis=0).astype(BF16))

    copies_w[1].wait()
    for z in range(2):
        o = corr(hext, w2, 128, z, False)
        out_ref[:, z * C : (z + 1) * C] = own_rows(o, 0).astype(BF16)

    for c in hid:
        c.wait_recv()

    @pl.loop(0, SLOTS)
    def _(s):
        acc = None
        for j in range(4):
            left = jnp.concatenate([hg[2 * j], hg[2 * j + 1]], axis=1)
            term = dot(left, rbuf[s, j * C : (j + 1) * C, :])
            acc = term if acc is None else acc + term
        for h in range(2):
            grad[h, pl.ds(pl.multiple_of(s * C, C), C), :] = acc[:, 128 * h : 128 * h + 128]

    def rows_of(j):
        return jnp.concatenate([grad[h, pl.ds(offset + ROWS * j, PAD), :] for h in range(2)], axis=1)

    def share(d):
        return pltpu.make_async_remote_copy(
            src_ref=chunk.at[d], dst_ref=land.at[d], send_sem=rsend.at[d], recv_sem=rrecv.at[d],
            device_id=at(0, d), device_id_type=MESH)

    @pl.loop(1, NGY)
    def _(d):
        j = lax.rem(gy + d, NGY)
        chunk[d] = rows_of(j).astype(BF16)
        share(d).start()

    for z in range(2):
        bk = corr(ext.at[1], w2, 160, z, True)
        p = pre[:, z * C : (z + 1) * C]
        sg = 1.0 / (1.0 + jnp.exp(-p))
        text[:, z * C : (z + 1) * C] = (bk * sg * (1.0 + p * (1.0 - sg))).astype(BF16)
    for z in range(2):
        o = corr(text, w1, 128, z, True)
        vg_ref[:, z * C : (z + 1) * C] = own_rows(o, 0).astype(BF16)

    sg_ref[...] = rows_of(gy)

    @pl.loop(1, NGY)
    def _(d):
        share(d).wait_recv()
        sg_ref[...] += land[d].astype(F32)

    sg_ref[...] = sg_ref[...] * np.float32(1.0 / np.sqrt(np.float32(32768.0)))

    @pl.loop(1, NGY)
    def _(d):
        share(d).wait_send()

    for c in halo[0] + halo[1] + craw + cstrip + hid:
        c.wait_send()


def body(volume, first_weight, second_weight, cotangent):
    vmem = pl.BlockSpec(memory_space=pltpu.VMEM)
    hbm = pl.BlockSpec(memory_space=pl.ANY)
    own, got = window_matrices()
    dma = pltpu.SemaphoreType.DMA
    scratch = [
        pltpu.VMEM((27 * C, C), BF16),
        pltpu.VMEM((27 * C, C), BF16),
        pltpu.VMEM((2, 96, 2 * C), BF16),
        pltpu.VMEM((2, 128, 2 * C), BF16),
        pltpu.VMEM((2, 192, 2 * C), BF16),
        pltpu.VMEM((160, 2 * C), BF16),
        pltpu.VMEM((160, 2 * C), BF16),
        pltpu.VMEM((160, 2 * C), F32),
        pltpu.VMEM((NGX, OWN, 2 * C), BF16),
        pltpu.VMEM((NGX, 32, 2 * C), BF16),
        pltpu.VMEM((2, 512, C), F32),
        pltpu.VMEM((2, 256, C), F32),
        pltpu.VMEM((NGX, C, 128), BF16),
        pltpu.VMEM((SLOTS, 1024, C), BF16),
        pltpu.VMEM((2, SLOTS * C, 128), F32),
        pltpu.VMEM((NGY, PAD, C), BF16),
        pltpu.VMEM((NGY, PAD, C), BF16),
        dma((2,)), dma((2, 8)), dma((2, 8)),
        dma((NGX,)), dma((NGX,)), dma((NGX,)), dma((NGX,)), dma((NGX,)), dma((NGX,)),
        dma((NGY,)), dma((NGY,)),
    ]
    out, vg, sg = pl.pallas_call(
        kernel,
        out_shape=(
            jax.ShapeDtypeStruct((OWN, 2 * C), BF16),
            jax.ShapeDtypeStruct((OWN, 2 * C), BF16),
            jax.ShapeDtypeStruct((PAD, C), F32),
        ),
        in_specs=[vmem, vmem, hbm, hbm, vmem, vmem, vmem],
        out_specs=(vmem, vmem, vmem),
        scratch_shapes=scratch,
        compiler_params=pltpu.CompilerParams(
            collective_id=0, has_side_effects=True, vmem_limit_bytes=48 * 2**20),
    )(
        volume.reshape(OWN, 2 * C), cotangent.reshape(OWN, 2 * C), first_weight, second_weight,
        jnp.asarray(strip_matrix(), BF16), jnp.asarray(own, BF16), jnp.asarray(got, BF16),
    )
    return out.reshape(volume.shape), vg.reshape(volume.shape), sg[:ROWS].reshape(-1)


def solution(mesh):
    in_specs = (P("gx", "gy", None, None), P(), P(), P("gx", "gy", None, None))
    out_specs = (P("gx", "gy", None, None), P("gx", "gy", None, None), P(("gx", "gy")))
    return jax.shard_map(body, mesh=mesh, in_specs=in_specs, out_specs=out_specs, check_vma=False)
```
